512 devices in a mesh: row: 32 (over z, core), col: 16 (over y, x).
Axes of the slice: x: 4, y: 4, z: 16, core: 2. Of those that a mesh axis runs over, the one named last changes fastest.
Arguments:
- gram: float32 [9, 512, 8, 8192], P(None, 'row', None, 'col'), may hold values from 0 to 4, as said below
Outputs:
- trailing: float32 [9, 512, 8, 8192], P(None, 'row', None, 'col')
- factor: float32 [8, 16, 512, 512], P(None, 'col', 'row')
The draws below stay inside these ranges and needn't reach their ends.
Inputs may be any that keep to these rules, and one draw needn't show every extreme that they name: gram holds the first 4608 rows of a symmetric positive definite 65536 x 65536 matrix whose smallest eigenvalue is at least 0.5.
All inputs are finite; a program needn't handle non-finite values.
Results may differ from the reference program's by a relative error of at most 0.0003.
Values sent between devices are 32-bit elements; how exact they have to be, the bound alone decides.
A program may use at most 64 MiB of HBM per device.

```python
import jax
import jax.numpy as jnp
from jax import lax

B = 512
SLAB = 9
TC = 8
ORDER = 65536
N_COL = 16


def draw_gram(key, part):
    key_points, key_jitter = jax.random.split(key)
    point_dims = 16
    points = jax.random.normal(key_points, (ORDER, point_dims), jnp.float32)
    jitter = jax.random.uniform(key_jitter, (SLAB * B,), jnp.float32, 1.0, 2.0)
    distance = jnp.zeros((SLAB * B, ORDER), jnp.float32)
    for feature in range(point_dims):
        offset = points[:SLAB * B, None, feature] - points[None, :, feature]
        distance = distance + offset * offset
    kernel = jnp.exp(-distance / (2.0 * point_dims))
    row_index = jnp.arange(SLAB * B)
    col_index = jnp.arange(ORDER)
    kernel = jnp.where(row_index[:, None] == col_index[None, :], kernel + jitter[:, None], kernel)
    return kernel.reshape(SLAB, B, TC, ORDER // TC)


def setup_inputs(seed: int = 0) -> dict:
    arg_keys = jax.random.split(jax.random.key(seed), 2)
    gram = draw_gram(jax.random.fold_in(arg_keys[1], 71), 0)
    return {"gram": gram}


def reference(gram):
    matrix = gram.reshape(SLAB * B, ORDER)
    diagonal = matrix[:B, :B]
    factor_tile = jnp.linalg.cholesky(diagonal)
    inverse = jax.scipy.linalg.solve_triangular(factor_tile, jnp.eye(B, dtype=jnp.float32), lower=True)
    across = jnp.dot(matrix[:B, :].T, inverse.T, precision=lax.Precision.HIGHEST)
    across = across.at[:B].set(factor_tile)
    solved = jnp.dot(matrix[:, :B], inverse.T, precision=lax.Precision.HIGHEST)
    solved = solved.at[:B].set(factor_tile)
    product = jnp.dot(solved[B:], across[B:].T, precision=lax.Precision.HIGHEST)
    lower_part = matrix[B:, B:] - product
    trailing = jnp.pad(lower_part, ((B, 0), (B, 0)))
    return (trailing.reshape(SLAB, B, TC, ORDER // TC), across.reshape(TC, N_COL, B, B))
```

```python
import functools

import jax
import jax.numpy as jnp
from jax import lax
from jax.experimental import pallas as pl
from jax.experimental.pallas import tpu as pltpu
from jax.sharding import PartitionSpec as P

F32 = jnp.float32
EXACT = lax.Precision.HIGHEST
MESH = pl.DeviceIdType.MESH
LANES = 128
GROUP = 8
CHUNKS = 4
EVENTS_PER_HOP = 2
RIGHT, LEFT, TWIN_RIGHT, TWIN_LEFT = 0, 1, 2, 3


def dot(a, b, a_dim, b_dim):
    return lax.dot_general(a, b, (((a_dim,), (b_dim,)), ((), ())), precision=EXACT, preferred_element_type=F32)


def factor_block(panels, between):
    count = len(panels)
    lane = lax.broadcasted_iota(jnp.int32, (GROUP, LANES), 1)
    sub = lax.broadcasted_iota(jnp.int32, (GROUP, LANES), 0)
    rows = list(panels)
    upper, inverse = [], []
    for j in range(count):
        first = GROUP * j

        def columns(i):
            return [jnp.broadcast_to(rows[i][:, first + k:first + k + 1], (GROUP, LANES)) for k in range(GROUP)]

        pivot_columns = columns(j)
        s = [[None] * GROUP for _ in range(GROUP)]
        for k in range(GROUP):
            for q in range(k, GROUP):
                s[k][q] = jnp.broadcast_to(pivot_columns[q][k:k + 1, :], (GROUP, LANES))
        inv = [None] * GROUP
        for k in range(GROUP):
            inv[k] = 1.0 / s[k][k]
            for q in range(k + 1, GROUP):
                m = s[k][q] * inv[k]
                for t in range(q, GROUP):
                    s[q][t] = s[q][t] - m * s[k][t]
        scale = s[0][0]
        for k in range(1, GROUP):
            scale = jnp.where(sub == k, s[k][k], scale)
        scale = lax.rsqrt(scale)

        def multipliers(cols):
            cols, ms = list(cols), []
            for k in range(GROUP):
                m = cols[k] * inv[k]
                ms.append(m)
                for q in range(k + 1, GROUP):
                    cols[q] = cols[q] - m * s[k][q]
            return ms

        inside = (lane >= first) & (lane < first + GROUP)
        own = multipliers(pivot_columns)
        row = jnp.where(inside, (lane - first == sub).astype(F32), rows[j])
        pivot_rows = []
        for k in range(GROUP):
            b = jnp.broadcast_to(row[k:k + 1, :], (GROUP, LANES))
            pivot_rows.append(b)
            if k < GROUP - 1:
                row = row - jnp.where(sub > k, own[k], 0.0) * b
        row = row * scale
        corner = jnp.zeros((GROUP, LANES), F32)
        for k in range(GROUP):
            for q in range(k, GROUP):
                corner = jnp.where((sub == k) & (lane == first + q), s[k][q], corner)
        upper.append(jnp.where(inside, corner * scale, jnp.where(lane >= first, row, 0.0)))
        inverse.append(jnp.where(lane < first + GROUP, row, 0.0))
        for i in range(j + 1, count):
            ms = multipliers(columns(i))
            r = jnp.where(inside, 0.0, rows[i])
            for k in range(GROUP):
                r = r - ms[k] * pivot_rows[k]
            rows[i] = r
        between(j)
    return upper, inverse


def kernel(nz, nx, ny, gram_ref, trailing_ref, factor_ref, whole_row, diagonal, z, corners, panel, picked,
           send_sem, ring_sem, twin_sem, spread_send, spread_recv):
    slab, part, tiles, size = gram_ref.shape
    blocks = size // LANES
    below = (slab - 1) * part
    row, col = lax.axis_index("row"), lax.axis_index("col")
    place, core = row // 2, row % 2
    x, y = col % nx, col // nx
    half = nz // 2
    width = tiles // CHUNKS
    d_chunk = CHUNKS

    def device(at_place, at_core, at_col):
        return (at_place * 2 + at_core, at_col)

    right = device((place + 1) % nz, core, col)
    left = device((place + nz - 1) % nz, core, col)
    sibling = device(place, 1 - core, col)

    mine = pl.ds(pl.multiple_of(row * part, part), part)
    for c in range(tiles):
        whole_row[c, mine, :] = gram_ref[0, :, c, :]

    @pl.when(col == 0)
    def _():
        diagonal[mine, :] = gram_ref[0, :, 0, :]
        for a in range(1, slab):
            panel[(a - 1) * part:a * part, :] = gram_ref[a, :, 0, :]

    barrier = pltpu.get_barrier_semaphore()
    for d in (right, left, sibling):
        pl.semaphore_signal(barrier, inc=1, device_id=d, device_id_type=MESH)

    @pl.when(y > 0)
    def _():
        pl.semaphore_signal(barrier, inc=1, device_id=(row, x), device_id_type=MESH)
        pl.semaphore_wait(barrier, 4)

    @pl.when(y == 0)
    def _():
        for other in range(1, ny):
            pl.semaphore_signal(barrier, inc=1, device_id=(row, other * nx + x), device_id_type=MESH)

        @pl.when(x > 0)
        def _():
            pl.semaphore_signal(barrier, inc=1, device_id=(row, 0), device_id_type=MESH)
            pl.semaphore_wait(barrier, 3 + ny)

        @pl.when(x == 0)
        def _():
            for other in range(1, nx):
                pl.semaphore_signal(barrier, inc=1, device_id=(row, other), device_id_type=MESH)
            pl.semaphore_wait(barrier, 1 + nx + ny)

    def shard(chunk, offset):
        rows = pl.ds(pl.multiple_of((((place + offset + nz) % nz) * 2 + core) * part, part), part)
        if chunk is None:
            return diagonal.at[rows, :]
        return whole_row.at[pl.ds(chunk * width, width), rows, :]

    def hop(chunk, offset, way):
        number = d_chunk if chunk is None else chunk
        seen = (offset + nz + {RIGHT: -1, LEFT: 1}.get(way, 0)) % nz
        target = {RIGHT: right, LEFT: left}.get(way, sibling)
        recv = (ring_sem if way in (RIGHT, LEFT) else twin_sem).at[number, seen]
        ref = shard(chunk, offset)
        return pltpu.make_async_remote_copy(src_ref=ref, dst_ref=ref, send_sem=send_sem.at[number, way], recv_sem=recv,
                                            device_id=target, device_id_type=MESH)

    def arrived(chunk, offset, twin=False):
        number = d_chunk if chunk is None else chunk
        sem = (twin_sem if twin else ring_sem).at[number, (offset + nz) % nz]
        ref = shard(chunk, offset)
        pltpu.make_async_remote_copy(src_ref=ref, dst_ref=ref, send_sem=send_sem.at[number, TWIN_RIGHT], recv_sem=sem,
                                     device_id=sibling, device_id_type=MESH).wait_recv()

    def begin(chunk):
        for way in (RIGHT, LEFT, TWIN_RIGHT):
            hop(chunk, 0, way).start()

    def onward(chunk, offset, way):
        copy = hop(chunk, offset, way)
        copy.wait_send()
        copy.start()

    def left_twin(chunk, step):
        copy = hop(chunk, step, TWIN_LEFT)

        @pl.when(step > 1)
        def _():
            copy.wait_send()

        copy.start()

    def spread(ref, number, slot, at_col):
        return pltpu.make_async_remote_copy(src_ref=ref, dst_ref=ref, send_sem=spread_send.at[number, slot],
                                            recv_sem=spread_recv.at[number], device_id=(row, at_col), device_id_type=MESH)

    d_mine = diagonal.at[mine, :]

    @pl.when(col == 0)
    def _():
        for other in range(1, nx):
            spread(d_mine, 0, other, other).start()

    @pl.when((y == 0) & (x > 0))
    def _():
        spread(d_mine, 0, 0, 0).wait_recv()

    @pl.when(y == 0)
    def _():
        for other in range(1, ny):
            spread(d_mine, 0, nx + other, other * nx + x).start()

    @pl.when(col == 0)
    def _():
        for other in range(1, nx):
            spread(panel, 1, other, other).start()

    for chunk in range(CHUNKS):
        begin(chunk)

    @pl.when(y > 0)
    def _():
        spread(d_mine, 0, 0, x).wait_recv()

    begin(None)

    def event(e):
        step, chunk = e // CHUNKS + 1, e % CHUNKS
        longer_right = chunk % 2 == 0

        @pl.when((step < half) | longer_right)
        def _():
            arrived(chunk, -step)

            @pl.when((step < half - 1) | ((step < half) & longer_right))
            def _():
                onward(chunk, -step, RIGHT)

            onward(chunk, -step, TWIN_RIGHT)

        @pl.when((step < half) | (chunk % 2 == 1))
        def _():
            arrived(chunk, step)

            @pl.when((step < half - 1) | ((step < half) & (chunk % 2 == 1)))
            def _():
                onward(chunk, step, LEFT)

            left_twin(chunk, step)

    def d_hop(step, carry):
        arrived(None, -step)

        @pl.when(step < half)
        def _():
            onward(None, -step, RIGHT)
            arrived(None, step)

            @pl.when(step < half - 1)
            def _():
                onward(None, step, LEFT)

            left_twin(None, step)

        onward(None, -step, TWIN_RIGHT)

        for n in range(EVENTS_PER_HOP):
            event((step - 1) * EVENTS_PER_HOP + n)
        return carry

    lax.fori_loop(1, half + 1, d_hop, 0)
    lax.fori_loop(0, nz, lambda i, carry: (arrived(None, i, True), carry)[1], 0)
    done = half * EVENTS_PER_HOP
    total = half * CHUNKS

    @pl.when((y == 0) & (x > 0))
    def _():
        spread(panel, 1, 0, 0).wait_recv()

    @pl.when(y == 0)
    def _():
        for other in range(1, ny):
            spread(panel, 1, nx + other, other * nx + x).start()

    z[...] = diagonal[...]
    per_block = (total - done) // blocks
    per_event = (LANES // GROUP) // per_block

    def block_step(kb, carry):
        start = pl.multiple_of(kb * LANES, LANES)

        def between(j):
            if j % per_event == per_event - 1:
                event(done + kb * per_block + j // per_event)

        panels = [z[pl.ds(start + GROUP * i, GROUP), pl.ds(start, LANES)] for i in range(LANES // GROUP)]
        upper, inverse = factor_block(panels, between)
        for i in range(LANES // GROUP):
            corners[kb, GROUP * i:GROUP * (i + 1), :] = upper[i]
            z[pl.ds(start + GROUP * i, GROUP), pl.ds(start, LANES)] = inverse[i]
        first = z[pl.ds(start, LANES), pl.ds(start, LANES)]
        for b in range(blocks):
            @pl.when(kb != b)
            def _():
                here = slice(b * LANES, (b + 1) * LANES)
                z[pl.ds(start, LANES), here] = dot(first, z[pl.ds(start, LANES), here], 1, 0)

        def update(ib, carry):
            low = pl.multiple_of(ib * LANES, LANES)
            u = z[pl.ds(start, LANES), pl.ds(low, LANES)]
            change = dot(u, z[pl.ds(start, LANES), :], 0, 0)
            keep = lax.broadcasted_iota(jnp.int32, (LANES, size), 1) // LANES != kb
            z[pl.ds(low, LANES), :] = jnp.where(keep, z[pl.ds(low, LANES), :], 0.0) - change
            return carry

        lax.fori_loop(kb + 1, blocks, update, 0)
        return carry

    lax.fori_loop(0, blocks, block_step, 0)

    own_first = row * part
    own_block = own_first // LANES
    own_lane = own_first % LANES
    aligned = pl.multiple_of(own_block * LANES, LANES)

    @pl.when(col == 0)
    def _():
        for b in range(blocks):
            here = slice(b * LANES, (b + 1) * LANES)
            values = jnp.where(b < own_block, z[here, pl.ds(aligned, LANES)], 0.0)
            values = jnp.where(b == own_block, corners[b], values)
            values = pltpu.roll(values, (LANES - own_lane) % LANES, 1)
            factor_ref[0, :, here] = values.T[:part, :]

    for b in range(blocks - 1):
        z[b * LANES:(b + 1) * LANES, (b + 1) * LANES:] = jnp.zeros((LANES, size - (b + 1) * LANES), F32)

    @pl.when(y > 0)
    def _():
        spread(panel, 1, 0, x).wait_recv()

    solved = dot(panel[...], z[...], 1, 1)
    weights = dot(solved, z[...], 1, 0)

    lane = lax.broadcasted_iota(jnp.int32, (size, LANES), 1)
    trailing_ref[0] = jnp.zeros((part, tiles, size), F32)
    for chunk in range(CHUNKS):
        lax.fori_loop(0, nz, lambda i, carry, chunk=chunk: (arrived(chunk, i, True), carry)[1], 0)
        for c in range(chunk * width, (chunk + 1) * width):
            tile = whole_row[c]
            change = dot(weights, tile, 1, 0)
            for a in range(1, slab):
                trailing_ref[a, :, c, :] = gram_ref[a, :, c, :] - change[(a - 1) * part:a * part, :]
            block = pltpu.roll(whole_row[c, :, pl.ds(aligned, LANES)], (c * part + LANES - own_lane) % LANES, 1)
            if c == 0:
                picked[...] = block
            else:
                picked[...] = jnp.where(lane // part == c, block, picked[...])
    across = dot(picked[...], z[...], 0, 1)

    @pl.when(col > 0)
    def _():
        factor_ref[0] = across[:part, :]

    for c in range(1, tiles):
        factor_ref[c] = across[c * part:(c + 1) * part, :]

    @pl.when(col == 0)
    def _():
        for a in range(1, slab):
            trailing_ref[a, :, 0, :] = jnp.zeros((part, size), F32)

    for chunk in (None,) + tuple(range(CHUNKS)):
        for way in (RIGHT, LEFT, TWIN_RIGHT, TWIN_LEFT):
            hop(chunk, 0, way).wait_send()

    @pl.when(y == 0)
    def _():
        @pl.when(x == 0)
        def _():
            for other in range(1, nx):
                spread(d_mine, 0, other, other).wait_send()
                spread(panel, 1, other, other).wait_send()
        for other in range(1, ny):
            spread(d_mine, 0, nx + other, other * nx + x).wait_send()
            spread(panel, 1, nx + other, other * nx + x).wait_send()


def body(gram, nz, nx, ny):
    slab, part, tiles, size = gram.shape
    blocks = size // LANES
    vmem = pl.BlockSpec(memory_space=pltpu.VMEM)
    trailing, factor = pl.pallas_call(
        functools.partial(kernel, nz, nx, ny),
        out_shape=(jax.ShapeDtypeStruct(gram.shape, F32), jax.ShapeDtypeStruct((tiles, part, size), F32)),
        in_specs=[vmem],
        out_specs=(vmem, vmem),
        scratch_shapes=[
            pltpu.VMEM((tiles, size, size), F32),
            pltpu.VMEM((size, size), F32),
            pltpu.VMEM((size, size), F32),
            pltpu.VMEM((blocks, LANES, LANES), F32),
            pltpu.VMEM(((slab - 1) * part, size), F32),
            pltpu.VMEM((size, LANES), F32),
            pltpu.SemaphoreType.DMA((CHUNKS + 1, 4)),
            pltpu.SemaphoreType.DMA((CHUNKS + 1, nz)),
            pltpu.SemaphoreType.DMA((CHUNKS + 1, nz)),
            pltpu.SemaphoreType.DMA((2, nx + ny)),
            pltpu.SemaphoreType.DMA((2,)),
        ],
        compiler_params=pltpu.CompilerParams(collective_id=0, has_side_effects=True, vmem_limit_bytes=40 << 20),
    )(gram)
    return trailing, factor[:, None]


def solution(mesh):
    nz = mesh.shape["row"] // 2
    nx = ny = int(round(mesh.shape["col"] ** 0.5))
    return jax.shard_map(
        functools.partial(body, nz=nz, nx=nx, ny=ny),
        mesh=mesh,
        in_specs=(P(None, "row", None, "col"),),
        out_specs=(P(None, "row", None, "col"), P(None, "col", "row", None)),
        check_vma=False,
    )
```

```python
import functools

import jax
import jax.numpy as jnp
from jax import lax
from jax.experimental import pallas as pl
from jax.experimental.pallas import tpu as pltpu
from jax.sharding import PartitionSpec as P

F32 = jnp.float32
EXACT = lax.Precision.HIGHEST
MESH = pl.DeviceIdType.MESH
LANES = 128
GROUP = 8
CHUNKS = 2
AFTER_SCATTER = 2
AFTER_ACROSS = 2
AFTER_EARLY = 2
RIGHT, LEFT, TWIN_RIGHT, TWIN_LEFT, TWIN_LAST = range(5)


def dot(a, b, a_dim, b_dim):
    return lax.dot_general(a, b, (((a_dim,), (b_dim,)), ((), ())), precision=EXACT, preferred_element_type=F32)


def factor_block(panels, between):
    count = len(panels)
    lane = lax.broadcasted_iota(jnp.int32, (GROUP, LANES), 1)
    sub = lax.broadcasted_iota(jnp.int32, (GROUP, LANES), 0)
    rows = list(panels)
    upper, inverse = [], []
    for j in range(count):
        first = GROUP * j

        def columns(i):
            return [jnp.broadcast_to(rows[i][:, first + k:first + k + 1], (GROUP, LANES)) for k in range(GROUP)]

        pivot_columns = columns(j)
        s = [[None] * GROUP for _ in range(GROUP)]
        for k in range(GROUP):
            for q in range(k, GROUP):
                s[k][q] = jnp.broadcast_to(pivot_columns[q][k:k + 1, :], (GROUP, LANES))
        inv = [None] * GROUP
        low = [[None] * GROUP for _ in range(GROUP)]
        for k in range(0, GROUP, 2):
            a, b, c = s[k][k], s[k][k + 1], s[k + 1][k + 1]
            r = 1.0 / (a * c - b * b)
            x, y = s[k], list(s[k + 1])
            for q in range(k + 2, GROUP):
                for t in range(q, GROUP):
                    change = x[q] * (c * x[t] - b * y[t]) + y[q] * (a * y[t] - b * x[t])
                    s[q][t] = s[q][t] - change * r
            inv[k] = 1.0 / a
            inv[k + 1] = a * r
            low[k + 1][k] = b * inv[k]
            for t in range(k + 1, GROUP):
                s[k + 1][t] = y[t] - low[k + 1][k] * x[t]
            for q in range(k + 2, GROUP):
                low[q][k] = x[q] * inv[k]
                low[q][k + 1] = s[k + 1][q] * inv[k + 1]
        scale = s[0][0]
        for k in range(1, GROUP):
            scale = jnp.where(sub == k, s[k][k], scale)
        scale = lax.rsqrt(scale)

        def multipliers(cols):
            cols, ms = list(cols), []
            for k in range(GROUP):
                m = cols[k] * inv[k]
                ms.append(m)
                for q in range(k + 1, GROUP):
                    cols[q] = cols[q] - m * s[k][q]
            return ms

        inside = (lane >= first) & (lane < first + GROUP)
        start = jnp.where(inside, (lane - first == sub).astype(F32), rows[j])
        pivot_rows = []
        for k in range(GROUP):
            b = jnp.broadcast_to(start[k:k + 1, :], (GROUP, LANES))
            for q in range(k):
                b = b - low[k][q] * pivot_rows[q]
            pivot_rows.append(b)
        row = pivot_rows[0]
        for k in range(1, GROUP):
            row = jnp.where(sub == k, pivot_rows[k], row)
        row = row * scale
        corner = jnp.zeros((GROUP, LANES), F32)
        for k in range(GROUP):
            for q in range(k, GROUP):
                corner = jnp.where((sub == k) & (lane == first + q), s[k][q], corner)
        upper.append(jnp.where(inside, corner * scale, jnp.where(lane >= first, row, 0.0)))
        inverse.append(jnp.where(lane < first + GROUP, row, 0.0))
        for i in range(j + 1, count):
            ms = multipliers(columns(i))
            r = jnp.where(inside, 0.0, rows[i])
            for k in range(GROUP):
                r = r - ms[k] * pivot_rows[k]
            rows[i] = r
        between(j)
    return upper, inverse


def when(condition, action):
    if isinstance(condition, bool):
        if condition:
            action()
    else:
        pl.when(condition)(action)


def kernel(nz, nx, ny, gram_hbm, trailing_ref, factor_ref, gram_ref, whole_row, source, tiles_of_d, z, corners, panel, picked,
           load_sem, send_sem, ring_sem, twin_sem, d_send, d_recv, spread_send, spread_recv):
    slab, part, tiles, size = gram_ref.shape
    blocks = size // LANES
    row, col = lax.axis_index("row"), lax.axis_index("col")
    place, core = row // 2, row % 2
    x, y = col % nx, col // nx
    cols = nx * ny
    half = nz // 2
    width = tiles // CHUNKS
    heights = part // GROUP
    per_core = heights * blocks
    early = nz // blocks

    def wrap(index, count):
        if isinstance(index, int):
            return index % count
        index = jnp.where(index >= count, index - count, index)
        return jnp.where(index < 0, index + count, index)

    def device(at_place, at_core, at_col):
        return (at_place * 2 + at_core, at_col)

    right = device(wrap(place + 1, nz), core, col)
    left = device(wrap(place - 1, nz), core, col)
    sibling = device(place, 1 - core, col)

    def repeat(count, step, first=0):
        for i in range(first, count):
            step(i)

    load_first = pltpu.make_async_copy(gram_hbm.at[0], gram_ref.at[0], load_sem.at[0])
    load_rest = pltpu.make_async_copy(gram_hbm.at[pl.ds(1, slab - 1)], gram_ref.at[pl.ds(1, slab - 1)], load_sem.at[1])
    load_first.start()
    load_rest.start()

    barrier = pltpu.get_barrier_semaphore()

    def greet(d):
        pl.semaphore_signal(barrier, inc=1, device_id=d, device_id_type=MESH)

    greet(sibling)
    repeat(nz, lambda i: greet(device(wrap(place + i, nz), core, col)), 1)
    repeat(cols, lambda i: greet((row, wrap(col + i, cols))), 1)

    load_first.wait()
    mine = pl.ds(pl.multiple_of(row * part, part), part)
    for c in range(tiles):
        whole_row[c, mine, :] = gram_ref[0, :, c, :]

    @pl.when(col == 0)
    def _():
        own = gram_ref[0, :, 0, :]
        for h in range(heights):
            for b in range(blocks):
                source[h * blocks + b] = own[h * GROUP:(h + 1) * GROUP, b * LANES:(b + 1) * LANES]

        @pl.when(core == 0)
        def _():
            tiles_of_d[place, 0] = own[:GROUP, :LANES]

    pl.semaphore_wait(barrier, nz + cols - 1)

    def shard(chunk, offset):
        rows = pl.ds(pl.multiple_of((wrap(place + offset, nz) * 2 + core) * part, part), part)
        tile = slice(None) if chunk is None else pl.ds(chunk * width, width)
        return whole_row.at[tile, rows, :]

    def copy_to(target, ref, send, recv):
        return pltpu.make_async_remote_copy(src_ref=ref, dst_ref=ref, send_sem=send, recv_sem=recv,
                                            device_id=target, device_id_type=MESH)

    def hop(chunk, offset, way):
        target, shift = (right, -1) if way == RIGHT else (left, 1)
        return copy_to(target, shard(chunk, offset), send_sem.at[chunk, way],
                       ring_sem.at[chunk, wrap(offset + shift, nz)])

    def twin(offset, way=TWIN_RIGHT):
        return copy_to(sibling, shard(None, offset), send_sem.at[0, way], twin_sem.at[0, wrap(offset, nz)])

    def last_twin(chunk):
        return copy_to(sibling, shard(chunk, half), send_sem.at[chunk, TWIN_LAST], twin_sem.at[chunk, half])

    def arrived(chunk, offset):
        copy_to(sibling, shard(chunk, offset), send_sem.at[chunk, TWIN_LAST],
                ring_sem.at[chunk, wrap(offset, nz)]).wait_recv()

    def onward(copy):
        copy.wait_send()
        copy.start()

    def event(number, later=0):
        step, chunk = number // CHUNKS + 1 + later, number % CHUNKS
        last_right, last_left = (half, half - 1) if chunk % 2 == 0 else (half - 1, half)

        def from_left():
            arrived(chunk, -step)
            when(step < last_right, lambda: onward(hop(chunk, -step, RIGHT)))

        def from_right():
            arrived(chunk, step)
            when(step < last_left, lambda: onward(hop(chunk, step, LEFT)))

        def twins():
            onward(twin(-step, TWIN_RIGHT))
            left_one = twin(step, TWIN_LEFT)
            when(step > 1, left_one.wait_send)
            left_one.start()

        when(step <= last_right, from_left)
        when(step <= last_left, from_right)
        if chunk == CHUNKS - 1:
            when(step < half, twins)
        when(step == half, lambda: last_twin(chunk).start())

    SCATTER, ACROSS, EARLY, LATE, TWIN_EARLY, TWIN_LATE = range(6)
    holder = col // per_core == core
    first_holder = core * per_core

    def d_copy(ref, kind, target):
        return pltpu.make_async_remote_copy(src_ref=ref, dst_ref=ref, send_sem=d_send.at[kind], recv_sem=d_recv.at[kind],
                                            device_id=target, device_id_type=MESH)

    def scatter(i):
        target = (row, first_holder + i)
        return pltpu.make_async_remote_copy(src_ref=source.at[i], dst_ref=tiles_of_d.at[place, first_holder + i],
                                            send_sem=d_send.at[SCATTER], recv_sem=d_recv.at[SCATTER],
                                            device_id=target, device_id_type=MESH)

    def tiles_at(p, t, planes=1, count=1):
        return tiles_of_d.at[pl.ds(p, planes), pl.ds(t, count)]

    one_tile = tiles_at(place, col)
    early_tiles = tiles_at(0, col, early)
    late_tiles = tiles_at(early, col, nz - early)

    @pl.when(col == 0)
    def _():
        @pl.when(core > 0)
        def _():
            scatter(0).start()

        for i in range(1, per_core):
            scatter(i).start()

    for chunk in range(CHUNKS):
        hop(chunk, 0, RIGHT).start()
        hop(chunk, 0, LEFT).start()
    twin(0).start()

    @pl.when(holder)
    def _():
        @pl.when(col > 0)
        def _():
            d_copy(one_tile, SCATTER, (row, 0)).wait_recv()

        repeat(nz, lambda i: d_copy(one_tile, ACROSS, device(wrap(place + i, nz), core, col)).start(), 1)

    events = [0]

    def take(count):
        for _ in range(count):
            event(events[0])
            events[0] += 1

    take(AFTER_SCATTER)

    @pl.when(holder)
    def _():
        d_copy(tiles_at(0, col, nz - 1), ACROSS, right).wait_recv()
        repeat(cols, lambda i: d_copy(early_tiles, EARLY, (row, wrap(col + i, cols))).start(), 1)

    take(AFTER_ACROSS)

    def take_plane(kind, twin_kind, p, planes):
        @pl.when(holder)
        def _():
            d_copy(tiles_at(p, 0, planes, per_core - 1), kind, sibling).wait_recv()

        @pl.when(jnp.logical_not(holder))
        def _():
            d_copy(tiles_at(p, 0, planes, per_core), kind, sibling).wait_recv()

        d_copy(tiles_at(p, first_holder, planes, per_core), twin_kind, sibling).start()

    take_plane(EARLY, TWIN_EARLY, 0, early)

    @pl.when(holder)
    def _():
        repeat(cols, lambda i: d_copy(late_tiles, LATE, (row, wrap(col + i, cols))).start(), 1)

    def spread(slot, at_col):
        return pltpu.make_async_remote_copy(src_ref=panel, dst_ref=panel, send_sem=spread_send.at[slot],
                                            recv_sem=spread_recv.at[0], device_id=(row, at_col), device_id_type=MESH)

    load_rest.wait()

    @pl.when(col == 0)
    def _():
        for a in range(1, slab):
            panel[(a - 1) * part:a * part, :] = gram_ref[a, :, 0, :]
        for other in range(1, nx):
            spread(other, other).start()

    take(AFTER_EARLY)
    d_copy(tiles_at(0, per_core - first_holder, early, per_core), TWIN_EARLY, sibling).wait_recv()

    def tile_rows(first, planes, write):
        for p in range(first, first + planes):
            for t in range(2 * per_core):
                r = (p * 2 + t // per_core) * part + (t % per_core) // blocks * GROUP
                write(slice(r, r + GROUP), slice(t % blocks * LANES, (t % blocks + 1) * LANES), tiles_of_d[p, t])

    def put(r, c, value):
        z[r, c] = value

    def add(r, c, value):
        if c.start >= LANES:
            z[r, c] = z[r, c] + value

    tile_rows(0, early, put)
    z[LANES:, :] = jnp.zeros((size - LANES, size), F32)

    done = events[0]
    total = half * CHUNKS
    per_block = CHUNKS
    groups = LANES // GROUP

    def panel_onward():
        @pl.when((y == 0) & (x > 0))
        def _():
            spread(0, 0).wait_recv()

        @pl.when(y == 0)
        def _():
            for other in range(1, ny):
                spread(nx + other, other * nx + x).start()

    def block_step(kb, carry):
        start = pl.multiple_of(kb * LANES, LANES)

        def between(j):
            for n in range(j * per_block // groups, (j + 1) * per_block // groups):
                event(done + n, kb)
            if j == groups // 2:
                pl.when(kb == 1)(panel_onward)

        @pl.when(kb == 1)
        def _():
            take_plane(LATE, TWIN_LATE, early, nz - early)
            d_copy(tiles_at(early, per_core - first_holder, nz - early, per_core), TWIN_LATE, sibling).wait_recv()
            tile_rows(early, nz - early, add)

        panels = [z[pl.ds(start + GROUP * i, GROUP), pl.ds(start, LANES)] for i in range(groups)]
        upper, inverse = factor_block(panels, between)
        for i in range(groups):
            corners[kb, GROUP * i:GROUP * (i + 1), :] = upper[i]
            z[pl.ds(start + GROUP * i, GROUP), pl.ds(start, LANES)] = inverse[i]
        first = z[pl.ds(start, LANES), pl.ds(start, LANES)]
        for b in range(blocks):
            @pl.when(kb != b)
            def _():
                here = slice(b * LANES, (b + 1) * LANES)
                z[pl.ds(start, LANES), here] = dot(first, z[pl.ds(start, LANES), here], 1, 0)

        def update(ib, carry):
            low = pl.multiple_of(ib * LANES, LANES)
            u = z[pl.ds(start, LANES), pl.ds(low, LANES)]
            change = dot(u, z[pl.ds(start, LANES), :], 0, 0)
            keep = lax.broadcasted_iota(jnp.int32, (LANES, size), 1) // LANES != kb
            z[pl.ds(low, LANES), :] = jnp.where(keep, z[pl.ds(low, LANES), :], 0.0) - change
            return carry

        lax.fori_loop(kb + 1, blocks, update, 0)
        return carry

    lax.fori_loop(0, blocks, block_step, 0)
    done = done + blocks * per_block

    own_first = row * part
    own_block = own_first // LANES
    own_lane = own_first % LANES
    aligned = pl.multiple_of(own_block * LANES, LANES)

    @pl.when(col == 0)
    def _():
        for b in range(blocks):
            here = slice(b * LANES, (b + 1) * LANES)
            values = jnp.where(b < own_block, z[here, pl.ds(aligned, LANES)], 0.0)
            values = jnp.where(b == own_block, corners[b], values)
            values = pltpu.roll(values, (LANES - own_lane) % LANES, 1)
            factor_ref[0, :, here] = values.T[:part, :]

    for b in range(blocks - 1):
        z[b * LANES:(b + 1) * LANES, (b + 1) * LANES:] = jnp.zeros((LANES, size - (b + 1) * LANES), F32)

    @pl.when(y > 0)
    def _():
        spread(0, x).wait_recv()

    solved = dot(panel[...], z[...], 1, 1)
    weights = dot(solved, z[...], 1, 0)

    lane = lax.broadcasted_iota(jnp.int32, (size, LANES), 1)
    trailing_ref[0] = jnp.zeros((part, tiles, size), F32)
    for e in range(done, total - CHUNKS):
        event(e)

    for i in range(nz):
        if i != half:
            twin(i).wait_recv()
    for chunk in range(CHUNKS):
        if done <= total - CHUNKS + chunk:
            event(total - CHUNKS + chunk)
        last_twin(chunk).wait_recv()
        for c in range(chunk * width, (chunk + 1) * width):
            tile = whole_row[c]
            change = dot(weights, tile, 1, 0)
            for a in range(1, slab):
                trailing_ref[a, :, c, :] = gram_ref[a, :, c, :] - change[(a - 1) * part:a * part, :]
            block = pltpu.roll(whole_row[c, :, pl.ds(aligned, LANES)], (c * part + LANES - own_lane) % LANES, 1)
            if c == 0:
                picked[...] = block
            else:
                picked[...] = jnp.where(lane // part == c, block, picked[...])
    across = dot(picked[...], z[...], 0, 1)

    @pl.when(col > 0)
    def _():
        factor_ref[0] = across[:part, :]

    for c in range(1, tiles):
        factor_ref[c] = across[c * part:(c + 1) * part, :]

    @pl.when(col == 0)
    def _():
        for a in range(1, slab):
            trailing_ref[a, :, 0, :] = jnp.zeros((part, size), F32)

    for chunk in range(CHUNKS):
        hop(chunk, 0, RIGHT).wait_send()
        hop(chunk, 0, LEFT).wait_send()
        last_twin(chunk).wait_send()
    twin(0, TWIN_RIGHT).wait_send()
    twin(0, TWIN_LEFT).wait_send()
    for kind, p, planes in ((TWIN_EARLY, 0, early), (TWIN_LATE, early, nz - early)):
        d_copy(tiles_at(p, first_holder, planes, per_core), kind, sibling).wait_send()

    @pl.when(holder)
    def _():
        d_copy(tiles_at(0, col, nz - 1), ACROSS, right).wait_send()
        d_copy(tiles_at(0, 0, early, cols - 1), EARLY, right).wait_send()
        d_copy(tiles_at(early, 0, nz - early, cols - 1), LATE, right).wait_send()

    @pl.when(col == 0)
    def _():
        @pl.when(core == 0)
        def _():
            d_copy(tiles_at(place, 0, 1, per_core - 1), SCATTER, right).wait_send()

        @pl.when(core == 1)
        def _():
            d_copy(tiles_at(place, 0, 1, per_core), SCATTER, right).wait_send()

        for other in range(1, nx):
            spread(other, other).wait_send()

    @pl.when(y == 0)
    def _():
        for other in range(1, ny):
            spread(nx + other, other * nx + x).wait_send()


def body(gram, nz, nx, ny):
    slab, part, tiles, size = gram.shape
    blocks = size // LANES
    vmem = pl.BlockSpec(memory_space=pltpu.VMEM)
    trailing, factor = pl.pallas_call(
        functools.partial(kernel, nz, nx, ny),
        out_shape=(jax.ShapeDtypeStruct(gram.shape, F32), jax.ShapeDtypeStruct((tiles, part, size), F32)),
        in_specs=[pl.BlockSpec(memory_space=pltpu.HBM)],
        out_specs=(vmem, vmem),
        scratch_shapes=[
            pltpu.VMEM(gram.shape, F32),
            pltpu.VMEM((tiles, size, size), F32),
            pltpu.VMEM((part // GROUP * blocks, GROUP, LANES), F32),
            pltpu.VMEM((nz, 2 * part // GROUP * blocks, GROUP, LANES), F32),
            pltpu.VMEM((size, size), F32),
            pltpu.VMEM((blocks, LANES, LANES), F32),
            pltpu.VMEM(((slab - 1) * part, size), F32),
            pltpu.VMEM((size, LANES), F32),
            pltpu.SemaphoreType.DMA((2,)),
            pltpu.SemaphoreType.DMA((CHUNKS, 5)),
            pltpu.SemaphoreType.DMA((CHUNKS, nz)),
            pltpu.SemaphoreType.DMA((CHUNKS, nz)),
            pltpu.SemaphoreType.DMA((6,)),
            pltpu.SemaphoreType.DMA((6,)),
            pltpu.SemaphoreType.DMA((nx + ny,)),
            pltpu.SemaphoreType.DMA((1,)),
        ],
        compiler_params=pltpu.CompilerParams(collective_id=0, has_side_effects=True, vmem_limit_bytes=40 << 20),
    )(gram)
    return trailing, factor[:, None]


def solution(mesh):
    nz = mesh.shape["row"] // 2
    nx = ny = int(round(mesh.shape["col"] ** 0.5))
    return jax.shard_map(
        functools.partial(body, nz=nz, nx=nx, ny=ny),
        mesh=mesh,
        in_specs=(P(None, "row", None, "col"),),
        out_specs=(P(None, "row", None, "col"), P(None, "col", "row", None)),
        check_vma=False,
    )
```

```python
import functools

import jax
import jax.numpy as jnp
from jax import lax
from jax.experimental import pallas as pl
from jax.experimental.pallas import tpu as pltpu
from jax.sharding import PartitionSpec as P

F32 = jnp.float32
EXACT = lax.Precision.HIGHEST
MESH = pl.DeviceIdType.MESH
LANES = 128
GROUP = 8
CHUNKS = 2
AFTER_SCATTER = 2
AFTER_ACROSS = 2
AFTER_EARLY = 2
RIGHT, LEFT, TWIN_RIGHT, TWIN_LEFT, TWIN_LAST = range(5)


def dot(a, b, a_dim, b_dim):
    return lax.dot_general(a, b, (((a_dim,), (b_dim,)), ((), ())), precision=EXACT, preferred_element_type=F32)


def factor_block(panels, between):
    count = len(panels)
    lane = lax.broadcasted_iota(jnp.int32, (GROUP, LANES), 1)
    sub = lax.broadcasted_iota(jnp.int32, (GROUP, LANES), 0)
    rows = list(panels)
    upper, inverse = [], []
    for j in range(count):
        first = GROUP * j

        def columns(i):
            return [jnp.broadcast_to(rows[i][:, first + k:first + k + 1], (GROUP, LANES)) for k in range(GROUP)]

        pivot_columns = columns(j)
        s = [[None] * GROUP for _ in range(GROUP)]
        for k in range(GROUP):
            for q in range(k, GROUP):
                s[k][q] = jnp.broadcast_to(pivot_columns[q][k:k + 1, :], (GROUP, LANES))
        inv = [None] * GROUP
        low = [[None] * GROUP for _ in range(GROUP)]
        for k in range(0, GROUP, 2):
            a, b, c = s[k][k], s[k][k + 1], s[k + 1][k + 1]
            r = 1.0 / (a * c - b * b)
            x, y = s[k], list(s[k + 1])
            for q in range(k + 2, GROUP):
                for t in range(q, GROUP):
                    change = x[q] * (c * x[t] - b * y[t]) + y[q] * (a * y[t] - b * x[t])
                    s[q][t] = s[q][t] - change * r
            inv[k] = 1.0 / a
            inv[k + 1] = a * r
            low[k + 1][k] = b * inv[k]
            for t in range(k + 1, GROUP):
                s[k + 1][t] = y[t] - low[k + 1][k] * x[t]
            for q in range(k + 2, GROUP):
                low[q][k] = x[q] * inv[k]
                low[q][k + 1] = s[k + 1][q] * inv[k + 1]
        scale = s[0][0]
        for k in range(1, GROUP):
            scale = jnp.where(sub == k, s[k][k], scale)
        scale = lax.rsqrt(scale)

        def multipliers(cols):
            cols, ms = list(cols), []
            for k in range(GROUP):
                m = cols[k] * inv[k]
                ms.append(m)
                for q in range(k + 1, GROUP):
                    cols[q] = cols[q] - m * s[k][q]
            return ms

        inside = (lane >= first) & (lane < first + GROUP)
        start = jnp.where(inside, (lane - first == sub).astype(F32), rows[j])
        pivot_rows = []
        for k in range(GROUP):
            b = jnp.broadcast_to(start[k:k + 1, :], (GROUP, LANES))
            for q in range(k):
                b = b - low[k][q] * pivot_rows[q]
            pivot_rows.append(b)
        row = pivot_rows[0]
        for k in range(1, GROUP):
            row = jnp.where(sub == k, pivot_rows[k], row)
        row = row * scale
        corner = jnp.zeros((GROUP, LANES), F32)
        for k in range(GROUP):
            for q in range(k, GROUP):
                corner = jnp.where((sub == k) & (lane == first + q), s[k][q], corner)
        upper.append(jnp.where(inside, corner * scale, jnp.where(lane >= first, row, 0.0)))
        inverse.append(jnp.where(lane < first + GROUP, row, 0.0))
        for i in range(j + 1, count):
            ms = multipliers(columns(i))
            r = jnp.where(inside, 0.0, rows[i])
            for k in range(GROUP):
                r = r - ms[k] * pivot_rows[k]
            rows[i] = r
        between(j)
    return upper, inverse


def when(condition, action):
    if isinstance(condition, bool):
        if condition:
            action()
    else:
        pl.when(condition)(action)


def kernel(nz, nx, ny, gram_hbm, trailing_ref, factor_ref, gram_ref, whole_row, source, tiles_of_d, z, corners, panel, picked,
           load_sem, send_sem, ring_sem, twin_sem, d_send, d_recv, spread_send, spread_recv):
    slab, part, tiles, size = gram_ref.shape
    blocks = size // LANES
    row, col = lax.axis_index("row"), lax.axis_index("col")
    place, core = row // 2, row % 2
    x, y = col % nx, col // nx
    cols = nx * ny
    half = nz // 2
    width = tiles // CHUNKS
    heights = part // GROUP
    per_core = heights * blocks
    early = nz // blocks

    def wrap(index, count):
        if isinstance(index, int):
            return index % count
        index = jnp.where(index >= count, index - count, index)
        return jnp.where(index < 0, index + count, index)

    def device(at_place, at_core, at_col):
        return (at_place * 2 + at_core, at_col)

    right = device(wrap(place + 1, nz), core, col)
    left = device(wrap(place - 1, nz), core, col)
    sibling = device(place, 1 - core, col)

    def repeat(count, step, first=0):
        for i in range(first, count):
            step(i)

    load_first = pltpu.make_async_copy(gram_hbm.at[0], gram_ref.at[0], load_sem.at[0])
    load_rest = pltpu.make_async_copy(gram_hbm.at[pl.ds(1, slab - 1)], gram_ref.at[pl.ds(1, slab - 1)], load_sem.at[1])
    load_first.start()
    load_rest.start()

    barrier = pltpu.get_barrier_semaphore()

    def greet(d):
        pl.semaphore_signal(barrier, inc=1, device_id=d, device_id_type=MESH)

    greet(sibling)
    repeat(nz, lambda i: greet(device(wrap(place + i, nz), core, col)), 1)
    repeat(cols, lambda i: greet((row, wrap(col + i, cols))), 1)

    load_first.wait()
    mine = pl.ds(pl.multiple_of(row * part, part), part)
    for c in range(tiles):
        whole_row[c, mine, :] = gram_ref[0, :, c, :]

    @pl.when(col == 0)
    def _():
        own = gram_ref[0, :, 0, :]
        for h in range(heights):
            for b in range(blocks):
                source[h * blocks + b] = own[h * GROUP:(h + 1) * GROUP, b * LANES:(b + 1) * LANES]

        @pl.when(core == 0)
        def _():
            tiles_of_d[place, 0] = own[:GROUP, :LANES]

    pl.semaphore_wait(barrier, nz + cols - 1)

    def shard(chunk, offset):
        rows = pl.ds(pl.multiple_of((wrap(place + offset, nz) * 2 + core) * part, part), part)
        tile = slice(None) if chunk is None else pl.ds(chunk * width, width)
        return whole_row.at[tile, rows, :]

    def copy_to(target, ref, send, recv):
        return pltpu.make_async_remote_copy(src_ref=ref, dst_ref=ref, send_sem=send, recv_sem=recv,
                                            device_id=target, device_id_type=MESH)

    def hop(chunk, offset, way):
        target, shift = (right, -1) if way == RIGHT else (left, 1)
        return copy_to(target, shard(chunk, offset), send_sem.at[chunk, way],
                       ring_sem.at[chunk, wrap(offset + shift, nz)])

    def twin(offset, way=TWIN_RIGHT):
        return copy_to(sibling, shard(None, offset), send_sem.at[0, way], twin_sem.at[0, wrap(offset, nz)])

    def last_twin(chunk):
        return copy_to(sibling, shard(chunk, half), send_sem.at[chunk, TWIN_LAST], twin_sem.at[chunk, half])

    def arrived(chunk, offset):
        copy_to(sibling, shard(chunk, offset), send_sem.at[chunk, TWIN_LAST],
                ring_sem.at[chunk, wrap(offset, nz)]).wait_recv()

    def onward(copy):
        copy.wait_send()
        copy.start()

    def event(number, later=0):
        step, chunk = number // CHUNKS + 1 + later, number % CHUNKS
        last_right, last_left = (half, half - 1) if chunk % 2 == 0 else (half - 1, half)

        def from_left():
            arrived(chunk, -step)
            when(step < last_right, lambda: onward(hop(chunk, -step, RIGHT)))

        def from_right():
            arrived(chunk, step)
            when(step < last_left, lambda: onward(hop(chunk, step, LEFT)))

        def twins():
            onward(twin(-step, TWIN_RIGHT))
            left_one = twin(step, TWIN_LEFT)
            when(step > 1, left_one.wait_send)
            left_one.start()

        when(step <= last_right, from_left)
        when(step <= last_left, from_right)
        if chunk == CHUNKS - 1:
            when(step < half, twins)
        when(step == half, lambda: last_twin(chunk).start())

    SCATTER, ACROSS, EARLY, LATE, TWIN_EARLY, TWIN_LATE = range(6)
    holder = col // per_core == core
    first_holder = core * per_core

    def d_copy(ref, kind, target):
        return pltpu.make_async_remote_copy(src_ref=ref, dst_ref=ref, send_sem=d_send.at[kind], recv_sem=d_recv.at[kind],
                                            device_id=target, device_id_type=MESH)

    def scatter(i):
        target = (row, first_holder + i)
        return pltpu.make_async_remote_copy(src_ref=source.at[i], dst_ref=tiles_of_d.at[place, first_holder + i],
                                            send_sem=d_send.at[SCATTER], recv_sem=d_recv.at[SCATTER],
                                            device_id=target, device_id_type=MESH)

    def tiles_at(p, t, planes=1, count=1):
        return tiles_of_d.at[pl.ds(p, planes), pl.ds(t, count)]

    one_tile = tiles_at(place, col)
    early_tiles = tiles_at(0, col, early)
    late_tiles = tiles_at(early, col, nz - early)

    @pl.when(col == 0)
    def _():
        @pl.when(core > 0)
        def _():
            scatter(0).start()

        for i in range(1, per_core):
            scatter(i).start()

    for chunk in range(CHUNKS):
        hop(chunk, 0, RIGHT).start()
        hop(chunk, 0, LEFT).start()
    twin(0).start()

    @pl.when(holder)
    def _():
        @pl.when(col > 0)
        def _():
            d_copy(one_tile, SCATTER, (row, 0)).wait_recv()

        repeat(nz, lambda i: d_copy(one_tile, ACROSS, device(wrap(place + i, nz), core, col)).start(), 1)

    events = [0]

    def take(count):
        for _ in range(count):
            event(events[0])
            events[0] += 1

    take(AFTER_SCATTER)

    @pl.when(holder)
    def _():
        d_copy(tiles_at(0, col, nz - 1), ACROSS, right).wait_recv()
        repeat(cols, lambda i: d_copy(early_tiles, EARLY, (row, wrap(col + i, cols))).start(), 1)

    take(AFTER_ACROSS)

    def take_plane(kind, twin_kind, p, planes):
        @pl.when(holder)
        def _():
            d_copy(tiles_at(p, 0, planes, per_core - 1), kind, sibling).wait_recv()

        @pl.when(jnp.logical_not(holder))
        def _():
            d_copy(tiles_at(p, 0, planes, per_core), kind, sibling).wait_recv()

        d_copy(tiles_at(p, first_holder, planes, per_core), twin_kind, sibling).start()

    take_plane(EARLY, TWIN_EARLY, 0, early)

    @pl.when(holder)
    def _():
        repeat(cols, lambda i: d_copy(late_tiles, LATE, (row, wrap(col + i, cols))).start(), 1)

    def spread(slot, at_col):
        return pltpu.make_async_remote_copy(src_ref=panel, dst_ref=panel, send_sem=spread_send.at[slot],
                                            recv_sem=spread_recv.at[0], device_id=(row, at_col), device_id_type=MESH)

    load_rest.wait()

    @pl.when(col == 0)
    def _():
        for a in range(1, slab):
            panel[(a - 1) * part:a * part, :] = gram_ref[a, :, 0, :]
        for other in range(1, nx):
            spread(other, other).start()

    take(AFTER_EARLY)
    d_copy(tiles_at(0, per_core - first_holder, early, per_core), TWIN_EARLY, sibling).wait_recv()

    def tile_rows(first, planes, write):
        for p in range(first, first + planes):
            for t in range(2 * per_core):
                r = (p * 2 + t // per_core) * part + (t % per_core) // blocks * GROUP
                write(slice(r, r + GROUP), slice(t % blocks * LANES, (t % blocks + 1) * LANES), tiles_of_d[p, t])

    def put(r, c, value):
        z[r, c] = value

    def add(r, c, value):
        if c.start >= LANES:
            z[r, c] = z[r, c] + value

    tile_rows(0, early, put)
    z[LANES:, :] = jnp.zeros((size - LANES, size), F32)

    done = events[0]
    total = half * CHUNKS
    per_block = CHUNKS
    groups = LANES // GROUP

    def panel_onward():
        @pl.when((y == 0) & (x > 0))
        def _():
            spread(0, 0).wait_recv()

        @pl.when(y == 0)
        def _():
            for other in range(1, ny):
                spread(nx + other, other * nx + x).start()

    def block_step(kb, carry):
        start = pl.multiple_of(kb * LANES, LANES)

        def between(j):
            for n in range(j * per_block // groups, (j + 1) * per_block // groups):
                event(done + n, kb)
            if j == groups // 2:
                pl.when(kb == 1)(panel_onward)

        @pl.when(kb == 1)
        def _():
            take_plane(LATE, TWIN_LATE, early, nz - early)
            d_copy(tiles_at(early, per_core - first_holder, nz - early, per_core), TWIN_LATE, sibling).wait_recv()
            tile_rows(early, nz - early, add)

        panels = [z[pl.ds(start + GROUP * i, GROUP), pl.ds(start, LANES)] for i in range(groups)]
        upper, inverse = factor_block(panels, between)
        for i in range(groups):
            corners[kb, GROUP * i:GROUP * (i + 1), :] = upper[i]
            z[pl.ds(start + GROUP * i, GROUP), pl.ds(start, LANES)] = inverse[i]
        first = z[pl.ds(start, LANES), pl.ds(start, LANES)]
        for b in range(blocks):
            @pl.when(kb != b)
            def _():
                here = slice(b * LANES, (b + 1) * LANES)
                z[pl.ds(start, LANES), here] = dot(first, z[pl.ds(start, LANES), here], 1, 0)

        def update(ib, carry):
            low = pl.multiple_of(ib * LANES, LANES)
            u = z[pl.ds(start, LANES), pl.ds(low, LANES)]
            change = dot(u, z[pl.ds(start, LANES), :], 0, 0)
            keep = lax.broadcasted_iota(jnp.int32, (LANES, size), 1) // LANES != kb
            z[pl.ds(low, LANES), :] = jnp.where(keep, z[pl.ds(low, LANES), :], 0.0) - change
            return carry

        lax.fori_loop(kb + 1, blocks, update, 0)
        return carry

    lax.fori_loop(0, blocks, block_step, 0)
    done = done + blocks * per_block

    own_first = row * part
    own_block = own_first // LANES
    own_lane = own_first % LANES
    aligned = pl.multiple_of(own_block * LANES, LANES)

    @pl.when(col == 0)
    def _():
        for b in range(blocks):
            here = slice(b * LANES, (b + 1) * LANES)
            values = jnp.where(b < own_block, z[here, pl.ds(aligned, LANES)], 0.0)
            values = jnp.where(b == own_block, corners[b], values)
            values = pltpu.roll(values, (LANES - own_lane) % LANES, 1)
            factor_ref[0, :, here] = values.T[:part, :]

    for b in range(blocks - 1):
        z[b * LANES:(b + 1) * LANES, (b + 1) * LANES:] = jnp.zeros((LANES, size - (b + 1) * LANES), F32)

    @pl.when(y > 0)
    def _():
        spread(0, x).wait_recv()

    solved = dot(panel[...], z[...], 1, 1)
    weights = dot(solved, z[...], 1, 0)

    lane = lax.broadcasted_iota(jnp.int32, (size, LANES), 1)
    trailing_ref[0] = jnp.zeros((part, tiles, size), F32)
    for e in range(done, total - CHUNKS):
        event(e)

    for i in range(nz):
        if i != half:
            twin(i).wait_recv()
    for chunk in range(CHUNKS):
        if done <= total - CHUNKS + chunk:
            event(total - CHUNKS + chunk)
        last_twin(chunk).wait_recv()
        for c in range(chunk * width, (chunk + 1) * width):
            tile = whole_row[c]
            change = dot(weights, tile, 1, 0)
            for a in range(1, slab):
                trailing_ref[a, :, c, :] = gram_ref[a, :, c, :] - change[(a - 1) * part:a * part, :]
            block = pltpu.roll(whole_row[c, :, pl.ds(aligned, LANES)], (c * part + LANES - own_lane) % LANES, 1)
            if c == 0:
                picked[...] = block
            else:
                picked[...] = jnp.where(lane // part == c, block, picked[...])
    across = dot(picked[...], z[...], 0, 1)

    @pl.when(col > 0)
    def _():
        factor_ref[0] = across[:part, :]

    for c in range(1, tiles):
        factor_ref[c] = across[c * part:(c + 1) * part, :]

    @pl.when(col == 0)
    def _():
        for a in range(1, slab):
            trailing_ref[a, :, 0, :] = jnp.zeros((part, size), F32)

    for chunk in range(CHUNKS):
        hop(chunk, 0, RIGHT).wait_send()
        hop(chunk, 0, LEFT).wait_send()
        last_twin(chunk).wait_send()
    twin(0, TWIN_RIGHT).wait_send()
    twin(0, TWIN_LEFT).wait_send()
    for kind, p, planes in ((TWIN_EARLY, 0, early), (TWIN_LATE, early, nz - early)):
        d_copy(tiles_at(p, first_holder, planes, per_core), kind, sibling).wait_send()

    @pl.when(holder)
    def _():
        d_copy(tiles_at(0, col, nz - 1), ACROSS, right).wait_send()
        d_copy(tiles_at(0, 0, early, cols - 1), EARLY, right).wait_send()
        d_copy(tiles_at(early, 0, nz - early, cols - 1), LATE, right).wait_send()

    @pl.when(col == 0)
    def _():
        @pl.when(core == 0)
        def _():
            d_copy(tiles_at(place, 0, 1, per_core - 1), SCATTER, right).wait_send()

        @pl.when(core == 1)
        def _():
            d_copy(tiles_at(place, 0, 1, per_core), SCATTER, right).wait_send()

        for other in range(1, nx):
            spread(other, other).wait_send()

    @pl.when(y == 0)
    def _():
        for other in range(1, ny):
            spread(nx + other, other * nx + x).wait_send()


def body(gram, nz, nx, ny):
    slab, part, tiles, size = gram.shape
    blocks = size // LANES
    vmem = pl.BlockSpec(memory_space=pltpu.VMEM)
    trailing, factor = pl.pallas_call(
        functools.partial(kernel, nz, nx, ny),
        out_shape=(jax.ShapeDtypeStruct(gram.shape, F32), jax.ShapeDtypeStruct((tiles, part, size), F32)),
        in_specs=[pl.BlockSpec(memory_space=pltpu.HBM)],
        out_specs=(vmem, vmem),
        scratch_shapes=[
            pltpu.VMEM(gram.shape, F32),
            pltpu.VMEM((tiles, size, size), F32),
            pltpu.VMEM((part // GROUP * blocks, GROUP, LANES), F32),
            pltpu.VMEM((nz, 2 * part // GROUP * blocks, GROUP, LANES), F32),
            pltpu.VMEM((size, size), F32),
            pltpu.VMEM((blocks, LANES, LANES), F32),
            pltpu.VMEM(((slab - 1) * part, size), F32),
            pltpu.VMEM((size, LANES), F32),
            pltpu.SemaphoreType.DMA((2,)),
            pltpu.SemaphoreType.DMA((CHUNKS, 5)),
            pltpu.SemaphoreType.DMA((CHUNKS, nz)),
            pltpu.SemaphoreType.DMA((CHUNKS, nz)),
            pltpu.SemaphoreType.DMA((6,)),
            pltpu.SemaphoreType.DMA((6,)),
            pltpu.SemaphoreType.DMA((nx + ny,)),
            pltpu.SemaphoreType.DMA((1,)),
        ],
        compiler_params=pltpu.CompilerParams(collective_id=0, has_side_effects=True, vmem_limit_bytes=50 << 20),
    )(gram)
    return trailing, factor[:, None]


def solution(mesh):
    nz = mesh.shape["row"] // 2
    nx = ny = int(round(mesh.shape["col"] ** 0.5))
    return jax.shard_map(
        functools.partial(body, nz=nz, nx=nx, ny=ny),
        mesh=mesh,
        in_specs=(P(None, "row", None, "col"),),
        out_specs=(P(None, "row", None, "col"), P(None, "col", "row", None)),
        check_vma=False,
    )
```
